32 devices in a mesh: groups: 2 (over y), ctx: 4 (over z), tm: 2 (over x), tp: 2 (over core).
Axes of the slice: x: 2, y: 2, z: 4, core: 2. Of those that a mesh axis runs over, the one named last changes fastest.
Arguments:
- tokens: bfloat16 [256, 8, 1024], P(('groups', 'tm'), 'ctx'), parts along dimension 0, may hold values from -6 to 6
- norm_gain: float32 [1024], replicated, may hold values from 0.1 to 1.9
- block_mask: int32 [4, 4, 4], P(('groups', 'tm'), 'ctx'), parts along dimension 0, may hold values from 0 to 1, as said below
- w_query: bfloat16 [1024, 1024], P('tm', 'tp'), may hold values from -1.25 to 1.25
- w_key: bfloat16 [1024, 1024], P('tm', 'tp'), may hold values from -1.25 to 1.25
- w_value: bfloat16 [1024, 1024], P('tm', 'tp'), may hold values from -0.1875 to 0.1875
- w_out: bfloat16 [1024, 1024], P('tp', 'tm'), may hold values from -0.1875 to 0.1875
- w_up: bfloat16 [1024, 2048], P('tm', 'tp'), may hold values from -0.1875 to 0.1875
- w_down: bfloat16 [2048, 1024], P('tp', 'tm'), may hold values from -0.125 to 0.125
- conv_weight: float32 [5, 1024], P(None, 'tp'), may hold values from -2.5 to 2.5
Outputs:
- denoised: bfloat16 [256, 8, 1024], P(('groups', 'tm'), 'ctx', 'tp'), parts along dimension 0
The draws below stay inside these ranges and needn't reach their ends.
There are 2 independent parts, one for each index of `groups`. The reference program is written for one: setup_inputs(seed, part) draws one part's arguments, and reference() takes and returns one part's arrays. A program takes and returns all parts, laid end to end along the dimension named above; an argument that names none is the same for every part. Nothing has to cross between parts.
Inputs may be any that keep to these rules, and one draw needn't show every extreme that they name: block_mask[w, i, i] is 1 for every window w and block i.
All inputs are finite; a program needn't handle non-finite values.
Results may differ from the reference program's by a relative error of at most 0.0076.
Values may be sent and summed in bfloat16 or wider, within the bound.
A program may use at most 64 MiB of HBM per device.

```python
import jax
import jax.numpy as jnp
from jax import lax

D = 1024
HEADS = 16
HEAD_DIM = 64
FF = 2048
KERNEL = 5
DAN_DEV = 2
FRAME_DEV = 64
DANCERS = 8
FRAMES = 128
N_CTX = 4
N_TM = 2


def draw_block_mask(key, part):
    first = jax.random.fold_in(key, 11)
    second = jax.random.fold_in(key, 23)
    levels = jax.random.randint(first, (N_TM, N_CTX, 1), 1, 10)
    rolls = jax.random.randint(second, (N_TM, N_CTX, N_CTX), 0, 10)
    allowed = (rolls < levels).astype(jnp.int32)
    diagonal = jnp.eye(N_CTX, dtype=jnp.int32)[None, :, :]
    return jnp.maximum(allowed, diagonal)


def draw_tokens(key, part):
    noise = jax.random.normal(jax.random.fold_in(key, 7), (FRAMES, DANCERS, D), jnp.float32)
    return jnp.clip(noise, -6.0, 6.0).astype(jnp.bfloat16)


def drawn_weight(key, salt):
    scale = D ** (-0.5)
    drawn = jax.random.normal(jax.random.fold_in(key, salt), (D, D), jnp.float32)
    return jnp.clip(drawn * scale, -6.0 * scale, 6.0 * scale)


def draw_w_query(key, part):
    return drawn_weight(key, 201).astype(jnp.bfloat16)


def draw_w_key(key, part):
    return drawn_weight(key, 202).astype(jnp.bfloat16)


def level_of(key, dims, cuts, low, largest):
    def one(position, blocks):
        steps = jax.random.uniform(jax.random.fold_in(jax.random.fold_in(key, 6), position), (blocks,), jnp.float32, low / len(cuts), largest / len(cuts))
        return jnp.repeat(jnp.exp(steps), dims[position] // blocks).reshape((-1,) + (1,) * (len(dims) - position - 1))

    level = one(*cuts[0])
    for cut in cuts[1:]:
        level = level * one(*cut)
    return level


def scatter_about(own_key, shape, spread, reach, split=(), held_as=jnp.bfloat16):
    values = jax.random.normal(own_key, shape, jnp.float32) * spread
    if len(split) > 0:
        values = level_of(own_key, shape, split, -0.22, 0.18) * values
    return jnp.clip(values, min=-reach, max=reach).astype(held_as)


def setup_inputs(seed: int = 0, part: int = 0) -> dict:
    key_of = jax.random.split(jax.random.key(seed), 11)
    own_keys = jax.random.split(jax.random.fold_in(key_of[10], part), 11)
    return {
        "tokens": draw_tokens(jax.random.fold_in(jax.random.fold_in(key_of[10], part), 71), part),
        "norm_gain": jnp.clip(1.0 + 0.18 * jax.random.normal(key_of[1], (D,), jnp.float32), 0.1, 1.9),
        "block_mask": draw_block_mask(jax.random.fold_in(jax.random.fold_in(key_of[10], part), 71), part),
        "w_query": draw_w_query(jax.random.fold_in(key_of[10], 71), part),
        "w_key": draw_w_key(jax.random.fold_in(key_of[10], 71), part),
        "w_value": scatter_about(key_of[5], (D, D), D ** -0.5, 0.1875, ((0, 2), (1, 2))),
        "w_out": scatter_about(key_of[6], (D, D), D ** -0.5, 0.1875, ((0, 2), (1, 2))),
        "w_up": scatter_about(key_of[7], (D, FF), D ** -0.5, 0.1875, ((0, 2), (1, 2))),
        "w_down": scatter_about(key_of[8], (FF, D), FF ** -0.5, 0.125, ((0, 2), (1, 2))),
        "conv_weight": scatter_about(key_of[9], (KERNEL, D), KERNEL ** -0.5, 2.5, ((1, 2),), jnp.float32),
    }


def rms_norm(tokens, norm_gain):
    values = tokens.astype(jnp.float32)
    square = lax.optimization_barrier(jnp.mean(values * values, axis=-1, keepdims=True))
    return (values * lax.rsqrt(square + 1e-05) * norm_gain).astype(jnp.bfloat16)

def reference(tokens, norm_gain, block_mask, w_query, w_key, w_value, w_out, w_up, w_down, conv_weight):
    normed = rms_norm(tokens, norm_gain)
    flat = normed.reshape(FRAMES * DANCERS, D)
    queries = jnp.dot(flat, w_query, preferred_element_type=jnp.float32).astype(jnp.bfloat16)
    keys = jnp.dot(flat, w_key, preferred_element_type=jnp.float32).astype(jnp.bfloat16)
    values = jnp.dot(flat, w_value, preferred_element_type=jnp.float32).astype(jnp.bfloat16)
    window_tokens = FRAME_DEV * DANCERS

    def split_heads(array):
        return array.reshape(N_TM, window_tokens, HEADS, HEAD_DIM).transpose(0, 2, 1, 3)
    blocks = jnp.arange(DANCERS) // DAN_DEV
    chooser = (blocks[:, None] == jnp.arange(N_CTX)[None, :]).astype(jnp.float32)

    def window(inputs):
        query_w, key_w, value_w, mask_w = inputs
        dancer_mask = jnp.dot(jnp.dot(chooser, mask_w.astype(jnp.float32)), chooser.T)
        allowed = jnp.tile(dancer_mask, (FRAME_DEV, FRAME_DEV))

        def one_head(head_inputs):
            head_q, head_k, head_v = head_inputs
            scores = jnp.dot(head_q, head_k.T, preferred_element_type=jnp.float32) * 0.125
            scores = jnp.where(allowed > 0, scores, -1e+30)
            peak = lax.optimization_barrier(jnp.max(scores, axis=-1, keepdims=True))
            expo = jnp.exp(scores - peak) * allowed
            total = lax.optimization_barrier(jnp.sum(expo, axis=-1, keepdims=True))
            probs = expo.astype(jnp.bfloat16)
            mixed = jnp.dot(probs, head_v, preferred_element_type=jnp.float32)
            return mixed / total
        return lax.map(one_head, (query_w, key_w, value_w))
    attended = lax.map(window, (split_heads(queries), split_heads(keys), split_heads(values), block_mask))
    attended = attended.transpose(0, 2, 1, 3).reshape(FRAMES * DANCERS, D).astype(jnp.bfloat16)
    hidden = jnp.dot(flat, w_up, preferred_element_type=jnp.float32)
    activated = jax.nn.gelu(hidden, approximate=True).astype(jnp.bfloat16)
    branches = jnp.dot(attended, w_out, preferred_element_type=jnp.float32)
    branches = branches + jnp.dot(activated, w_down, preferred_element_type=jnp.float32)
    padded = jnp.pad(normed.astype(jnp.float32), ((2, 2), (0, 0), (0, 0)))
    convolved = jnp.zeros((FRAMES, DANCERS, D), jnp.float32)
    for offset in range(KERNEL):
        convolved = convolved + conv_weight[offset] * padded[offset:offset + FRAMES]
    total_out = tokens.astype(jnp.float32) + branches.reshape(FRAMES, DANCERS, D) + convolved
    return total_out.astype(jnp.bfloat16)
```

```python
import functools

import jax
import jax.numpy as jnp
from jax import lax
from jax.experimental import pallas as pl
from jax.experimental.pallas import tpu as pltpu
from jax.sharding import PartitionSpec as P

HEAD_DIM = 64
KERNEL = 5


def from_behind(value, axis, steps):
    count = lax.axis_size(axis)
    first, last = (max(0, -steps), min(count, count - steps))
    return lax.ppermute(value, axis, [(source, source + steps) for source in range(first, last)])


def rms_norm(tokens, norm_gain):
    values = tokens.astype(jnp.float32)
    square = jnp.mean(values * values, axis=-1, keepdims=True)
    return (values * lax.rsqrt(square + 1e-05) * norm_gain).astype(jnp.bfloat16)


def on_device(
    tokens, norm_gain, block_mask, w_query, w_key, w_value, w_out, w_up, w_down, conv_weight
):
    frames_here, dancers_here, width = tokens.shape
    rows_here = frames_here * dancers_here
    normed_grid = rms_norm(tokens, norm_gain)
    normed = normed_grid.reshape(rows_here, width)
    pieces = (
        lax.all_gather(w_query, "tm", axis=0, tiled=True),
        lax.all_gather(w_key, "tm", axis=0, tiled=True),
        lax.all_gather(w_value, "tm", axis=0, tiled=True),
        lax.all_gather(w_up, "tm", axis=0, tiled=True),
    )
    query_sum, key_sum, value_sum, hidden = tuple(
        (jnp.dot(normed, piece_one, preferred_element_type=jnp.float32) for piece_one in pieces)
    )
    local_heads = query_sum.shape[1] // HEAD_DIM
    queries = query_sum.astype(jnp.bfloat16).reshape(rows_here, local_heads, HEAD_DIM)
    key_grid = key_sum.astype(jnp.bfloat16).reshape(
        frames_here, dancers_here, local_heads * HEAD_DIM
    )
    value_grid = value_sum.astype(jnp.bfloat16).reshape(
        frames_here, dancers_here, local_heads * HEAD_DIM
    )
    mask_row = block_mask[0, 0].astype(jnp.float32)
    cycle_blocks = mask_row.shape[0]
    key_piece = lax.all_gather(key_grid, "ctx", axis=1, tiled=True)
    value_piece = lax.all_gather(value_grid, "ctx", axis=1, tiled=True)
    count = key_piece.shape[1]
    block_ids = jnp.arange(count) // dancers_here
    picker = (block_ids[:, None] == jnp.arange(cycle_blocks)[None, :]).astype(jnp.float32)
    allowed_dancers = jnp.dot(picker, mask_row)
    peak_old = jnp.full((local_heads, rows_here), -1e30, jnp.float32)
    key_rows = key_piece.reshape(frames_here * count, local_heads, HEAD_DIM)
    value_rows = value_piece.reshape(frames_here * count, local_heads, HEAD_DIM)
    allowed = jnp.tile(allowed_dancers, frames_here)
    scores = (
        jnp.einsum("qhd,khd->hqk", queries, key_rows, preferred_element_type=jnp.float32) * 0.125
    )
    scores = jnp.where(allowed[None, None, :] > 0, scores, -1e30)
    peak_new = jnp.maximum(peak_old, jnp.max(scores, axis=-1))
    expo = jnp.exp(scores - peak_new[:, :, None]) * allowed[None, None, :]
    total_new = jnp.sum(expo, axis=-1)
    probs = expo.astype(jnp.bfloat16)
    mixed_new = jnp.einsum("hqk,khd->hqd", probs, value_rows, preferred_element_type=jnp.float32)
    attended = (
        (mixed_new / total_new[:, :, None])
        .transpose(1, 0, 2)
        .reshape(rows_here, local_heads * HEAD_DIM)
        .astype(jnp.bfloat16)
    )
    activated = jax.nn.gelu(hidden, approximate=True).astype(jnp.bfloat16)
    out_full, down_full = (
        lax.all_gather(w_out, "tm", axis=1, tiled=True),
        lax.all_gather(w_down, "tm", axis=1, tiled=True),
    )
    branches = jnp.dot(attended, out_full, preferred_element_type=jnp.float32)
    branches = branches + jnp.dot(activated, down_full, preferred_element_type=jnp.float32)
    mine = lax.psum_scatter(
        branches.astype(jnp.bfloat16), "tp", scatter_dimension=1, tiled=True
    ).astype(jnp.float32)
    features_here = mine.shape[1]
    first_feature = lax.axis_index("tp") * features_here
    normed_cols = lax.dynamic_slice_in_dim(normed_grid, first_feature, features_here, 2)
    padded = jnp.pad(normed_cols.astype(jnp.float32), ((4, 4), (0, 0), (0, 0)))
    extended = jnp.zeros((frames_here + 4, dancers_here, features_here), jnp.float32)
    for offset in range(KERNEL):
        extended = extended + conv_weight[offset] * padded[offset : offset + frames_here + 4]
    convolved = extended[2 : frames_here + 2]
    from_before = from_behind(extended[frames_here + 2 :], "tm", 1)
    from_after = from_behind(extended[0:2], "tm", -1)
    convolved = convolved.at[0:2].add(from_before)
    convolved = convolved.at[frames_here - 2 :].add(from_after)
    token_cols = lax.dynamic_slice_in_dim(tokens, first_feature, features_here, 2).astype(
        jnp.float32
    )
    result = token_cols + mine.reshape(frames_here, dancers_here, features_here) + convolved
    return result.astype(jnp.bfloat16)


MESH = pl.DeviceIdType.MESH


def normalised(values, gain):
    values = values.astype(jnp.float32)
    square = jnp.mean(values * values, axis=-1, keepdims=True)
    return (values * lax.rsqrt(square + 1e-05) * gain).astype(jnp.bfloat16)


def layer_kernel(
    n_ctx,
    frame,
    mask_ref,
    tokens_ref,
    gain_ref,
    conv_ref,
    wq_ref,
    wk_ref,
    wv_ref,
    wup_ref,
    wout_ref,
    wdown_ref,
    out_ref,
    tok_all,
    normed,
    halo,
    halo_normed,
    bias,
    w_in,
    w_back,
    qkv,
    feats,
    theirs,
    sibling,
    mine,
    summed,
    arrived,
    extended,
    local_sem,
    tok_send,
    tok_recv,
    fwd_send,
    fwd_recv,
    bias_send,
    bias_recv,
    x_send,
    x_recv,
    y_send,
    y_recv,
    halo_sem,
    sib_send,
    sib_recv,
    red_send,
    red_recv,
):
    g = lax.axis_index("groups")
    c = lax.axis_index("ctx")
    i = lax.axis_index("tm")
    j = lax.axis_index("tp")
    rows, width = tokens_ref.shape
    half_rows = rows // 2
    depth = wq_ref.shape[0]
    part = depth // 2
    hw = wq_ref.shape[1] // n_ctx
    fw = wup_ref.shape[1] // n_ctx
    cols = out_ref.shape[1]
    heads = hw // HEAD_DIM
    to_x = {"tm": 1 - i}
    to_y = {"groups": 1 - g}
    to_tp = {"tp": 1 - j}

    def ahead(step):
        return lax.rem(c + step, n_ctx)

    def behind(step):
        return lax.rem(c + n_ctx - step, n_ctx)

    pieces = []
    for block in range(n_ctx):
        term = (mask_ref[0, block].astype(jnp.float32) - 1.0) * 1e30
        pieces.append(jnp.full((8, rows), term, jnp.float32))
    bias[c] = jnp.concatenate(pieces, axis=1)

    barrier = pltpu.get_barrier_semaphore()
    for peer in (to_x, to_y, to_tp):
        pl.semaphore_signal(barrier, inc=1, device_id=peer, device_id_type=MESH)
    for step in range(1, n_ctx):
        pl.semaphore_signal(
            barrier, inc=1, device_id={"ctx": ahead(step)}, device_id_type=MESH
        )

    def rows_at(start, size):
        return pl.ds(pl.multiple_of(start, 16), size)

    def cols_at(start, size):
        return pl.ds(pl.multiple_of(start, 128), size)

    def slices(first, count, owner):
        out = []
        for index, ref in enumerate((wq_ref, wk_ref, wv_ref)):
            out.append(
                (
                    ref.at[rows_at(first * depth // 2, count * part), cols_at(c * hw, hw)],
                    w_in.at[
                        rows_at(owner * depth + first * part, count * part),
                        index * hw : (index + 1) * hw,
                    ],
                )
            )
        out.append(
            (
                wup_ref.at[rows_at(first * part, count * part), cols_at(c * fw, fw)],
                w_in.at[
                    rows_at(owner * depth + first * part, count * part),
                    3 * hw : 3 * hw + fw,
                ],
            )
        )
        out.append(
            (
                wout_ref.at[rows_at(c * hw + first * (hw // 2), count * (hw // 2)), :],
                w_back.at[
                    rows_at(first * (hw // 2), count * (hw // 2)),
                    cols_at(owner * cols, cols),
                ],
            )
        )
        out.append(
            (
                wdown_ref.at[rows_at(c * fw + first * (fw // 2), count * (fw // 2)), :],
                w_back.at[
                    rows_at(hw + first * (fw // 2), count * (fw // 2)),
                    cols_at(owner * cols, cols),
                ],
            )
        )
        return out

    local = [
        pltpu.make_async_copy(source, target, local_sem.at[index])
        for index, (source, target) in enumerate(slices(0, 2, i))
    ]
    local.append(
        pltpu.make_async_copy(
            tokens_ref, tok_all.at[rows_at(c * rows, rows)], local_sem.at[6]
        )
    )
    for copy in local:
        copy.start()
    pl.semaphore_wait(barrier, n_ctx + 2)

    def remote(source, target, send, recv, peer):
        return pltpu.make_async_remote_copy(
            src_ref=source,
            dst_ref=target,
            send_sem=send,
            recv_sem=recv,
            device_id=peer,
            device_id_type=MESH,
        )

    x_out = [
        remote(source, target, x_send.at[index], x_recv.at[index], to_x)
        for index, (source, target) in enumerate(slices(g, 1, i))
    ]
    x_in = [
        remote(source, target, x_send.at[index], x_recv.at[index], to_x)
        for index, (source, target) in enumerate(slices(g, 1, 1 - i))
    ]
    halo_copy = remote(
        tokens_ref.at[rows_at((1 - i) * (rows - 16), 16)],
        halo,
        halo_sem.at[0],
        halo_sem.at[1],
        to_x,
    )

    def token_half(block, half):
        return tok_all.at[rows_at(block * rows + half * half_rows, half_rows)]

    tok_out, tok_in, fwd_out, fwd_in, bias_out, bias_in = [], [], [], [], [], []
    for step in range(1, n_ctx):
        peer = {"ctx": ahead(step)}
        at = step - 1
        own_half = tokens_ref.at[rows_at(j * half_rows, half_rows)]
        tok_out.append(
            remote(own_half, token_half(c, j), tok_send.at[at], tok_recv.at[at], peer)
        )
        source = behind(step)
        tok_in.append(
            remote(own_half, token_half(source, j), tok_send.at[at], tok_recv.at[at], peer)
        )
        fwd_out.append(
            remote(
                token_half(source, j), token_half(source, j), fwd_send.at[at], fwd_recv.at[at], to_tp
            )
        )
        fwd_in.append(
            remote(
                token_half(source, 1 - j),
                token_half(source, 1 - j),
                fwd_send.at[at],
                fwd_recv.at[at],
                to_tp,
            )
        )
        bias_out.append(remote(bias.at[c], bias.at[c], bias_send.at[at], bias_recv.at[at], peer))
        bias_in.append(
            remote(bias.at[source], bias.at[source], bias_send.at[at], bias_recv.at[at], peer)
        )

    def y_regions(half):
        other = 1 - i
        return [
            w_in.at[rows_at(other * depth + half * part, part), 0 : 3 * hw],
            w_in.at[rows_at(other * depth + half * part, part), 3 * hw : 3 * hw + fw],
            w_back.at[rows_at(half * (hw // 2), hw // 2), cols_at(other * cols, cols)],
            w_back.at[rows_at(hw + half * (fw // 2), fw // 2), cols_at(other * cols, cols)],
        ]

    y_out = [
        remote(region, region, y_send.at[index], y_recv.at[index], to_y)
        for index, region in enumerate(y_regions(g))
    ]
    y_in = [
        remote(region, region, y_send.at[index], y_recv.at[index], to_y)
        for index, region in enumerate(y_regions(1 - g))
    ]

    for copy in tok_out:
        copy.start()
    for copy in x_out[:4]:
        copy.start()
    halo_copy.start()
    for copy in x_out[4:]:
        copy.start()
    for copy in bias_out:
        copy.start()

    gain = gain_ref[...]

    def norm_block(block):
        at = rows_at(block * rows, rows)
        normed[at, :] = normalised(tok_all[at, :], gain)

    local[6].wait()
    norm_block(c)

    tok_in[0].wait_recv()
    fwd_out[0].start()
    for copy in x_in[:3]:
        copy.wait_recv()
    y_out[0].start()
    for at in range(1, n_ctx - 1):
        tok_in[at].wait_recv()
        fwd_out[at].start()
        fwd_in[at - 1].wait_recv()
        norm_block(behind(at))
    x_in[3].wait_recv()
    y_out[1].start()
    fwd_in[n_ctx - 2].wait_recv()
    norm_block(behind(n_ctx - 1))

    for copy in local[:4]:
        copy.wait()
    y_in[0].wait_recv()

    @pl.loop(0, n_ctx)
    def _(block):
        at = rows_at(block * rows, rows)
        qkv[at, :] = jnp.dot(
            normed[at, :], w_in[:, 0 : 3 * hw], preferred_element_type=jnp.float32
        ).astype(jnp.bfloat16)

    x_in[4].wait_recv()
    y_out[2].start()
    x_in[5].wait_recv()
    y_out[3].start()
    for copy in bias_in:
        copy.wait_recv()

    @pl.loop(0, n_ctx)
    def _(block):
        at = rows_at(block * rows, rows)
        outs = []
        for head in range(heads):
            low = head * HEAD_DIM
            query = qkv[at, low : low + HEAD_DIM]
            key = qkv[:, hw + low : hw + low + HEAD_DIM]
            value = qkv[:, 2 * hw + low : 2 * hw + low + HEAD_DIM]
            scores = lax.dot_general(
                query, key, (((1,), (1,)), ((), ())), preferred_element_type=jnp.float32
            )
            scores = scores * 0.125 + bias[block][0:1, :]
            peak = jnp.max(scores, axis=-1, keepdims=True)
            expo = jnp.exp(scores - peak)
            total = jnp.sum(expo, axis=-1, keepdims=True)
            mixed = jnp.dot(
                expo.astype(jnp.bfloat16), value, preferred_element_type=jnp.float32
            )
            outs.append(mixed / total)
        feats[at, 0:hw] = jnp.concatenate(outs, axis=1).astype(jnp.bfloat16)

    y_in[1].wait_recv()

    @pl.loop(0, n_ctx)
    def _(block):
        at = rows_at(block * rows, rows)
        hidden = jnp.dot(
            normed[at, :], w_in[:, 3 * hw : 3 * hw + fw], preferred_element_type=jnp.float32
        )
        feats[at, hw : hw + fw] = jax.nn.gelu(hidden, approximate=True).astype(jnp.bfloat16)

    for copy in local[4:6]:
        copy.wait()
    y_in[2].wait_recv()
    y_in[3].wait_recv()

    order = list(range(1, n_ctx)) + [0]
    sib_out, sib_in = [], []
    for index, step in enumerate(order):
        at = rows_at(ahead(step) * rows, rows)
        copy = remote(
            theirs.at[at], sibling.at[at], sib_send.at[index], sib_recv.at[index], to_tp
        )
        sib_out.append(copy)
        theirs[at, :] = jnp.dot(
            feats[at, :], w_back[:, cols_at((1 - j) * cols, cols)], preferred_element_type=jnp.float32
        ).astype(jnp.bfloat16)
        copy.start()
    for index, step in enumerate(order):
        at = rows_at(ahead(step) * rows, rows)
        mine[at, :] = jnp.dot(
            feats[at, :], w_back[:, cols_at(j * cols, cols)], preferred_element_type=jnp.float32
        )
    red = []
    for index, step in enumerate(order[:-1]):
        at = rows_at(ahead(step) * rows, rows)
        sib_out[index].wait_recv()
        summed[step - 1] = (mine[at, :] + sibling[at, :].astype(jnp.float32)).astype(jnp.bfloat16)
        copy = remote(
            summed.at[step - 1],
            arrived.at[step - 1],
            red_send.at[step - 1],
            red_recv.at[step - 1],
            {"ctx": ahead(step)},
        )
        copy.start()
        red.append(copy)

    halo_copy.wait_recv()
    halo_normed[...] = normalised(halo[...], gain)
    edge = halo_normed[:, cols_at(j * cols, cols)].astype(jnp.float32)
    own = rows_at(c * rows, rows)
    my_cols = cols_at(j * cols, cols)
    reach = KERNEL // 2
    before = jnp.where(i == 1, edge[8:16], 0.0)
    after = jnp.where(i == 0, edge[0:8], 0.0)
    extended[0:8, :] = before
    extended[8 : 8 + rows, :] = normed[own, my_cols].astype(jnp.float32)
    extended[8 + rows : 16 + rows, :] = after
    base = tokens_ref[:, my_cols].astype(jnp.float32)
    for tap in range(KERNEL):
        shift = 8 + (tap - reach) * frame
        base = base + conv_ref[tap : tap + 1, :] * extended[shift : shift + rows, :]
    sib_out[n_ctx - 1].wait_recv()
    base = base + mine[own, :] + sibling[own, :].astype(jnp.float32)
    for copy in red:
        copy.wait_recv()
    for step in range(n_ctx - 1):
        base = base + arrived[step].astype(jnp.float32)
    out_ref[...] = base.astype(out_ref.dtype)

    for copy in tok_out + x_out + [halo_copy] + bias_out + fwd_out + y_out + sib_out + red:
        copy.wait_send()


def in_one_kernel(
    n_ctx, tokens, norm_gain, block_mask, w_query, w_key, w_value, w_out, w_up, w_down, conv_weight
):
    frames_here, dancers_here, width = tokens.shape
    rows = frames_here * dancers_here
    cols = w_out.shape[1]
    hw = w_query.shape[1] // n_ctx
    fw = w_up.shape[1] // n_ctx
    depth = w_query.shape[0]
    every = n_ctx * rows
    bf16, f32 = jnp.bfloat16, jnp.float32
    vmem = pl.BlockSpec(memory_space=pltpu.VMEM)
    hbm = pl.BlockSpec(memory_space=pl.ANY)
    dma = pltpu.SemaphoreType.DMA
    out = pl.pallas_call(
        functools.partial(layer_kernel, n_ctx, dancers_here),
        out_shape=jax.ShapeDtypeStruct((rows, cols), bf16),
        in_specs=[pl.BlockSpec(memory_space=pltpu.SMEM)] + [vmem] * 3 + [hbm] * 6,
        out_specs=vmem,
        scratch_shapes=[
            pltpu.VMEM((every, width), bf16),
            pltpu.VMEM((every, width), bf16),
            pltpu.VMEM((16, width), bf16),
            pltpu.VMEM((16, width), bf16),
            pltpu.VMEM((n_ctx, 8, every), f32),
            pltpu.VMEM((2 * depth, 3 * hw + fw), bf16),
            pltpu.VMEM((hw + fw, 2 * cols), bf16),
            pltpu.VMEM((every, 3 * hw), bf16),
            pltpu.VMEM((every, hw + fw), bf16),
            pltpu.VMEM((every, cols), bf16),
            pltpu.VMEM((every, cols), bf16),
            pltpu.VMEM((every, cols), f32),
            pltpu.VMEM((n_ctx - 1, rows, cols), bf16),
            pltpu.VMEM((n_ctx - 1, rows, cols), bf16),
            pltpu.VMEM((rows + 16, cols), f32),
            dma((7,)),
            dma((n_ctx - 1,)),
            dma((n_ctx - 1,)),
            dma((n_ctx - 1,)),
            dma((n_ctx - 1,)),
            dma((n_ctx - 1,)),
            dma((n_ctx - 1,)),
            dma((6,)),
            dma((6,)),
            dma((4,)),
            dma((4,)),
            dma((2,)),
            dma((n_ctx,)),
            dma((n_ctx,)),
            dma((n_ctx - 1,)),
            dma((n_ctx - 1,)),
        ],
        compiler_params=pltpu.CompilerParams(
            collective_id=0, has_side_effects=True, vmem_limit_bytes=40 << 20
        ),
    )(
        block_mask[0],
        tokens.reshape(rows, width),
        norm_gain[None],
        conv_weight,
        w_query,
        w_key,
        w_value,
        w_up,
        w_out,
        w_down,
    )
    return out.reshape(frames_here, dancers_here, cols)


def solution(mesh):
    def body(tokens, norm_gain, block_mask, w_query, *rest):
        n_ctx = mesh.shape["ctx"]
        pairs = all(mesh.shape[axis] == 2 for axis in ("groups", "tm", "tp"))
        split = w_query.shape[1] % (128 * n_ctx) == 0 and tokens.shape[1] * (KERNEL // 2) <= 8
        if pairs and split and n_ctx > 2:
            return in_one_kernel(n_ctx, tokens, norm_gain, block_mask, w_query, *rest)
        return on_device(tokens, norm_gain, block_mask, w_query, *rest)

    placed = (
        P(("groups", "tm"), "ctx", None),
        P(),
        P(("groups", "tm"), "ctx", None),
        P("tm", "tp"),
        P("tm", "tp"),
        P("tm", "tp"),
        P("tp", "tm"),
        P("tm", "tp"),
        P("tp", "tm"),
        P(None, "tp"),
    )
    return jax.shard_map(
        body,
        mesh=mesh,
        in_specs=placed,
        out_specs=P(("groups", "tm"), "ctx", "tp"),
        check_vma=False,
    )
```

```python
import functools

import jax
import jax.numpy as jnp
from jax import lax
from jax.experimental import pallas as pl
from jax.experimental.pallas import tpu as pltpu
from jax.sharding import PartitionSpec as P

HEAD_DIM = 64
KERNEL = 5


def from_behind(value, axis, steps):
    count = lax.axis_size(axis)
    first, last = (max(0, -steps), min(count, count - steps))
    return lax.ppermute(value, axis, [(source, source + steps) for source in range(first, last)])


def rms_norm(tokens, norm_gain):
    values = tokens.astype(jnp.float32)
    square = jnp.mean(values * values, axis=-1, keepdims=True)
    return (values * lax.rsqrt(square + 1e-05) * norm_gain).astype(jnp.bfloat16)


def on_device(
    tokens, norm_gain, block_mask, w_query, w_key, w_value, w_out, w_up, w_down, conv_weight
):
    frames_here, dancers_here, width = tokens.shape
    rows_here = frames_here * dancers_here
    normed_grid = rms_norm(tokens, norm_gain)
    normed = normed_grid.reshape(rows_here, width)
    pieces = (
        lax.all_gather(w_query, "tm", axis=0, tiled=True),
        lax.all_gather(w_key, "tm", axis=0, tiled=True),
        lax.all_gather(w_value, "tm", axis=0, tiled=True),
        lax.all_gather(w_up, "tm", axis=0, tiled=True),
    )
    query_sum, key_sum, value_sum, hidden = tuple(
        (jnp.dot(normed, piece_one, preferred_element_type=jnp.float32) for piece_one in pieces)
    )
    local_heads = query_sum.shape[1] // HEAD_DIM
    queries = query_sum.astype(jnp.bfloat16).reshape(rows_here, local_heads, HEAD_DIM)
    key_grid = key_sum.astype(jnp.bfloat16).reshape(
        frames_here, dancers_here, local_heads * HEAD_DIM
    )
    value_grid = value_sum.astype(jnp.bfloat16).reshape(
        frames_here, dancers_here, local_heads * HEAD_DIM
    )
    mask_row = block_mask[0, 0].astype(jnp.float32)
    cycle_blocks = mask_row.shape[0]
    key_piece = lax.all_gather(key_grid, "ctx", axis=1, tiled=True)
    value_piece = lax.all_gather(value_grid, "ctx", axis=1, tiled=True)
    count = key_piece.shape[1]
    block_ids = jnp.arange(count) // dancers_here
    picker = (block_ids[:, None] == jnp.arange(cycle_blocks)[None, :]).astype(jnp.float32)
    allowed_dancers = jnp.dot(picker, mask_row)
    peak_old = jnp.full((local_heads, rows_here), -1e30, jnp.float32)
    key_rows = key_piece.reshape(frames_here * count, local_heads, HEAD_DIM)
    value_rows = value_piece.reshape(frames_here * count, local_heads, HEAD_DIM)
    allowed = jnp.tile(allowed_dancers, frames_here)
    scores = (
        jnp.einsum("qhd,khd->hqk", queries, key_rows, preferred_element_type=jnp.float32) * 0.125
    )
    scores = jnp.where(allowed[None, None, :] > 0, scores, -1e30)
    peak_new = jnp.maximum(peak_old, jnp.max(scores, axis=-1))
    expo = jnp.exp(scores - peak_new[:, :, None]) * allowed[None, None, :]
    total_new = jnp.sum(expo, axis=-1)
    probs = expo.astype(jnp.bfloat16)
    mixed_new = jnp.einsum("hqk,khd->hqd", probs, value_rows, preferred_element_type=jnp.float32)
    attended = (
        (mixed_new / total_new[:, :, None])
        .transpose(1, 0, 2)
        .reshape(rows_here, local_heads * HEAD_DIM)
        .astype(jnp.bfloat16)
    )
    activated = jax.nn.gelu(hidden, approximate=True).astype(jnp.bfloat16)
    out_full, down_full = (
        lax.all_gather(w_out, "tm", axis=1, tiled=True),
        lax.all_gather(w_down, "tm", axis=1, tiled=True),
    )
    branches = jnp.dot(attended, out_full, preferred_element_type=jnp.float32)
    branches = branches + jnp.dot(activated, down_full, preferred_element_type=jnp.float32)
    mine = lax.psum_scatter(
        branches.astype(jnp.bfloat16), "tp", scatter_dimension=1, tiled=True
    ).astype(jnp.float32)
    features_here = mine.shape[1]
    first_feature = lax.axis_index("tp") * features_here
    normed_cols = lax.dynamic_slice_in_dim(normed_grid, first_feature, features_here, 2)
    padded = jnp.pad(normed_cols.astype(jnp.float32), ((4, 4), (0, 0), (0, 0)))
    extended = jnp.zeros((frames_here + 4, dancers_here, features_here), jnp.float32)
    for offset in range(KERNEL):
        extended = extended + conv_weight[offset] * padded[offset : offset + frames_here + 4]
    convolved = extended[2 : frames_here + 2]
    from_before = from_behind(extended[frames_here + 2 :], "tm", 1)
    from_after = from_behind(extended[0:2], "tm", -1)
    convolved = convolved.at[0:2].add(from_before)
    convolved = convolved.at[frames_here - 2 :].add(from_after)
    token_cols = lax.dynamic_slice_in_dim(tokens, first_feature, features_here, 2).astype(
        jnp.float32
    )
    result = token_cols + mine.reshape(frames_here, dancers_here, features_here) + convolved
    return result.astype(jnp.bfloat16)


MESH = pl.DeviceIdType.MESH


def normalised(values, gain):
    values = values.astype(jnp.float32)
    square = jnp.mean(values * values, axis=-1, keepdims=True)
    return (values * lax.rsqrt(square + 1e-05) * gain).astype(jnp.bfloat16)


def layer_kernel(
    n_ctx,
    frame,
    mask_ref,
    tokens_hbm,
    gain_hbm,
    conv_hbm,
    wq_ref,
    wk_ref,
    wv_ref,
    wup_ref,
    wout_ref,
    wdown_ref,
    out_ref,
    gain_ref,
    conv_ref,
    tok_all,
    normed,
    halo,
    halo_normed,
    bias,
    w_in,
    w_back,
    qkv,
    feats,
    theirs,
    sibling,
    mine,
    summed,
    arrived,
    extended,
    local_sem,
    tok_send,
    tok_recv,
    fwd_send,
    fwd_recv,
    bias_send,
    bias_recv,
    x_send,
    x_recv,
    y_send,
    y_recv,
    halo_sem,
    sib_send,
    sib_recv,
    red_send,
    red_recv,
):
    g = lax.axis_index("groups")
    c = lax.axis_index("ctx")
    i = lax.axis_index("tm")
    j = lax.axis_index("tp")
    rows, width = tokens_hbm.shape
    half_rows = rows // 2
    depth = wq_ref.shape[0]
    part = depth // 2
    hw = wq_ref.shape[1] // n_ctx
    fw = wup_ref.shape[1] // n_ctx
    cols = out_ref.shape[1]
    heads = hw // HEAD_DIM
    to_x = {"tm": 1 - i}
    to_y = {"groups": 1 - g}
    to_tp = {"tp": 1 - j}

    def ahead(step):
        return lax.rem(c + step, n_ctx)

    def behind(step):
        return lax.rem(c + n_ctx - step, n_ctx)

    pieces = []
    for block in range(n_ctx):
        term = (mask_ref[0, block].astype(jnp.float32) - 1.0) * 1e30
        pieces.append(jnp.full((8, rows), term, jnp.float32))
    bias[c] = jnp.concatenate(pieces, axis=1)

    barrier = pltpu.get_barrier_semaphore()
    for peer in (to_x, to_y, to_tp):
        pl.semaphore_signal(barrier, inc=1, device_id=peer, device_id_type=MESH)
    for step in range(1, n_ctx):
        pl.semaphore_signal(
            barrier, inc=1, device_id={"ctx": ahead(step)}, device_id_type=MESH
        )

    def rows_at(start, size):
        return pl.ds(pl.multiple_of(start, 16), size)

    def cols_at(start, size):
        return pl.ds(pl.multiple_of(start, 128), size)

    def slices(first, count, owner):
        out = []
        for index, ref in enumerate((wq_ref, wk_ref, wv_ref)):
            out.append(
                (
                    ref.at[rows_at(first * depth // 2, count * part), cols_at(c * hw, hw)],
                    w_in.at[
                        rows_at(owner * depth + first * part, count * part),
                        index * hw : (index + 1) * hw,
                    ],
                )
            )
        out.append(
            (
                wup_ref.at[rows_at(first * part, count * part), cols_at(c * fw, fw)],
                w_in.at[
                    rows_at(owner * depth + first * part, count * part),
                    3 * hw : 3 * hw + fw,
                ],
            )
        )
        out.append(
            (
                wout_ref.at[rows_at(c * hw + first * (hw // 2), count * (hw // 2)), :],
                w_back.at[
                    rows_at(first * (hw // 2), count * (hw // 2)),
                    cols_at(owner * cols, cols),
                ],
            )
        )
        out.append(
            (
                wdown_ref.at[rows_at(c * fw + first * (fw // 2), count * (fw // 2)), :],
                w_back.at[
                    rows_at(hw + first * (fw // 2), count * (fw // 2)),
                    cols_at(owner * cols, cols),
                ],
            )
        )
        return out

    local = [
        pltpu.make_async_copy(source, target, local_sem.at[index])
        for index, (source, target) in enumerate(slices(0, 2, i))
    ]
    local.append(
        pltpu.make_async_copy(
            tokens_hbm, tok_all.at[rows_at(c * rows, rows)], local_sem.at[6]
        )
    )
    local.append(pltpu.make_async_copy(gain_hbm, gain_ref, local_sem.at[7]))
    local.append(pltpu.make_async_copy(conv_hbm, conv_ref, local_sem.at[8]))
    for copy in local:
        copy.start()
    pl.semaphore_wait(barrier, n_ctx + 2)

    def remote(source, target, send, recv, peer):
        return pltpu.make_async_remote_copy(
            src_ref=source,
            dst_ref=target,
            send_sem=send,
            recv_sem=recv,
            device_id=peer,
            device_id_type=MESH,
        )

    x_out = [
        remote(source, target, x_send.at[index], x_recv.at[index], to_x)
        for index, (source, target) in enumerate(slices(g, 1, i))
    ]
    x_in = [
        remote(source, target, x_send.at[index], x_recv.at[index], to_x)
        for index, (source, target) in enumerate(slices(g, 1, 1 - i))
    ]
    halo_copy = remote(
        tokens_hbm.at[rows_at((1 - i) * (rows - 16), 16)],
        halo,
        halo_sem.at[0],
        halo_sem.at[1],
        to_x,
    )

    def token_half(block, half):
        return tok_all.at[rows_at(block * rows + half * half_rows, half_rows)]

    tok_out, tok_in, fwd_out, fwd_in, bias_out, bias_in = [], [], [], [], [], []
    for step in range(1, n_ctx):
        peer = {"ctx": ahead(step)}
        at = step - 1
        own_half = tokens_hbm.at[rows_at(j * half_rows, half_rows)]
        tok_out.append(
            remote(own_half, token_half(c, j), tok_send.at[at], tok_recv.at[at], peer)
        )
        source = behind(step)
        tok_in.append(
            remote(own_half, token_half(source, j), tok_send.at[at], tok_recv.at[at], peer)
        )
        fwd_out.append(
            remote(
                token_half(source, j), token_half(source, j), fwd_send.at[at], fwd_recv.at[at], to_tp
            )
        )
        fwd_in.append(
            remote(
                token_half(source, 1 - j),
                token_half(source, 1 - j),
                fwd_send.at[at],
                fwd_recv.at[at],
                to_tp,
            )
        )
        bias_out.append(remote(bias.at[c], bias.at[c], bias_send.at[at], bias_recv.at[at], peer))
        bias_in.append(
            remote(bias.at[source], bias.at[source], bias_send.at[at], bias_recv.at[at], peer)
        )

    def y_copies(half):
        return [
            remote(target, target, y_send.at[index], y_recv.at[index], to_y)
            for index, (_, target) in enumerate(slices(half, 1, 1 - i))
        ]

    y_out, y_in = y_copies(g), y_copies(1 - g)

    steps = [2, 1] + list(range(3, n_ctx))
    for step in steps:
        tok_out[step - 1].start()
    for copy in x_out[:4]:
        copy.start()
    halo_copy.start()
    for copy in x_out[4:]:
        copy.start()
    for copy in bias_out:
        copy.start()

    local[7].wait()
    gain = gain_ref[...]

    def norm_block(block):
        at = rows_at(block * rows, rows)
        normed[at, :] = normalised(tok_all[at, :], gain)

    local[6].wait()
    norm_block(c)

    def pass_on(index):
        x_in[index].wait_recv()
        y_out[index].start()

    def share(step):
        tok_in[step - 1].wait_recv()
        fwd_out[step - 1].start()

    def settle(step):
        fwd_in[step - 1].wait_recv()
        norm_block(behind(step))

    def project(block):
        at = rows_at(block * rows, rows)
        qkv[at, :] = jnp.dot(
            normed[at, :], w_in[:, 0 : 3 * hw], preferred_element_type=jnp.float32
        ).astype(jnp.bfloat16)

    def feed(block):
        at = rows_at(block * rows, rows)
        hidden = jnp.dot(
            normed[at, :], w_in[:, 3 * hw : 3 * hw + fw], preferred_element_type=jnp.float32
        )
        feats[at, hw : hw + fw] = jax.nn.gelu(hidden, approximate=True).astype(jnp.bfloat16)

    def attend(block):
        at = rows_at(block * rows, rows)
        outs = []
        for head in range(heads):
            low = head * HEAD_DIM
            query = qkv[at, low : low + HEAD_DIM]
            key = qkv[:, hw + low : hw + low + HEAD_DIM]
            value = qkv[:, 2 * hw + low : 2 * hw + low + HEAD_DIM]
            scores = lax.dot_general(
                query, key, (((1,), (1,)), ((), ())), preferred_element_type=jnp.float32
            )
            scores = scores * 0.125 + bias[block][0:1, :]
            peak = jnp.max(scores, axis=-1, keepdims=True)
            expo = jnp.exp(scores - peak)
            total = jnp.sum(expo, axis=-1, keepdims=True)
            mixed = jnp.dot(
                expo.astype(jnp.bfloat16), value, preferred_element_type=jnp.float32
            )
            outs.append(mixed / total)
        feats[at, 0:hw] = jnp.concatenate(outs, axis=1).astype(jnp.bfloat16)

    pass_on(0)
    pass_on(1)
    pass_on(2)
    share(steps[0])
    pass_on(3)
    share(steps[1])
    settle(steps[0])
    for copy in local[:4]:
        copy.wait()
    for copy in y_in[:3]:
        copy.wait_recv()
    project(c)
    pass_on(4)
    project(behind(steps[0]))
    settle(steps[1])
    project(behind(steps[1]))
    y_in[3].wait_recv()
    feed(c)
    pass_on(5)
    for step in steps[2:]:
        share(step)
    feed(behind(steps[0]))
    feed(behind(steps[1]))
    for step in steps[2:]:
        settle(step)
        project(behind(step))
        feed(behind(step))
    for copy in bias_in:
        copy.wait_recv()
    for copy in local[4:6]:
        copy.wait()

    order = steps + [0]
    sib, red = [], []

    def reduce(index):
        step = order[index]
        at = rows_at(ahead(step) * rows, rows)
        sib[index].wait_recv()
        summed[step - 1] = (mine[at, :] + sibling[at, :].astype(jnp.float32)).astype(jnp.bfloat16)
        copy = remote(
            summed.at[step - 1],
            arrived.at[step - 1],
            red_send.at[step - 1],
            red_recv.at[step - 1],
            {"ctx": ahead(step)},
        )
        copy.start()
        red.append(copy)

    for index, step in enumerate(order):
        block = ahead(step)
        at = rows_at(block * rows, rows)
        attend(block)
        if index == 0:
            y_in[4].wait_recv()
            y_in[5].wait_recv()
        theirs[at, :] = jnp.dot(
            feats[at, :], w_back[:, cols_at((1 - j) * cols, cols)], preferred_element_type=jnp.float32
        ).astype(jnp.bfloat16)
        copy = remote(
            theirs.at[at], sibling.at[at], sib_send.at[index], sib_recv.at[index], to_tp
        )
        copy.start()
        sib.append(copy)
        mine[at, :] = jnp.dot(
            feats[at, :], w_back[:, cols_at(j * cols, cols)], preferred_element_type=jnp.float32
        )
        if index < n_ctx - 1:
            reduce(index)

    local[8].wait()
    halo_copy.wait_recv()
    halo_normed[...] = normalised(halo[...], gain)
    edge = halo_normed[:, cols_at(j * cols, cols)].astype(jnp.float32)
    own = rows_at(c * rows, rows)
    my_cols = cols_at(j * cols, cols)
    reach = KERNEL // 2
    before = jnp.where(i == 1, edge[8:16], 0.0)
    after = jnp.where(i == 0, edge[0:8], 0.0)
    extended[0:8, :] = before
    extended[8 : 8 + rows, :] = normed[own, my_cols].astype(jnp.float32)
    extended[8 + rows : 16 + rows, :] = after
    base = tok_all[own, my_cols].astype(jnp.float32)
    for tap in range(KERNEL):
        shift = 8 + (tap - reach) * frame
        base = base + conv_ref[tap : tap + 1, :] * extended[shift : shift + rows, :]
    sib[n_ctx - 1].wait_recv()
    base = base + mine[own, :] + sibling[own, :].astype(jnp.float32)
    for copy in red:
        copy.wait_recv()
    for step in range(n_ctx - 1):
        base = base + arrived[step].astype(jnp.float32)
    out_ref[...] = base.astype(out_ref.dtype)

    for copy in tok_out + x_out + [halo_copy] + bias_out + fwd_out + y_out + sib + red:
        copy.wait_send()


def in_one_kernel(
    n_ctx, tokens, norm_gain, block_mask, w_query, w_key, w_value, w_out, w_up, w_down, conv_weight
):
    frames_here, dancers_here, width = tokens.shape
    rows = frames_here * dancers_here
    cols = w_out.shape[1]
    hw = w_query.shape[1] // n_ctx
    fw = w_up.shape[1] // n_ctx
    depth = w_query.shape[0]
    every = n_ctx * rows
    bf16, f32 = jnp.bfloat16, jnp.float32
    vmem = pl.BlockSpec(memory_space=pltpu.VMEM)
    hbm = pl.BlockSpec(memory_space=pl.ANY)
    dma = pltpu.SemaphoreType.DMA
    out = pl.pallas_call(
        functools.partial(layer_kernel, n_ctx, dancers_here),
        out_shape=jax.ShapeDtypeStruct((rows, cols), bf16),
        in_specs=[pl.BlockSpec(memory_space=pltpu.SMEM)] + [hbm] * 9,
        out_specs=vmem,
        scratch_shapes=[
            pltpu.VMEM((1, width), f32),
            pltpu.VMEM(conv_weight.shape, f32),
            pltpu.VMEM((every, width), bf16),
            pltpu.VMEM((every, width), bf16),
            pltpu.VMEM((16, width), bf16),
            pltpu.VMEM((16, width), bf16),
            pltpu.VMEM((n_ctx, 8, every), f32),
            pltpu.VMEM((2 * depth, 3 * hw + fw), bf16),
            pltpu.VMEM((hw + fw, 2 * cols), bf16),
            pltpu.VMEM((every, 3 * hw), bf16),
            pltpu.VMEM((every, hw + fw), bf16),
            pltpu.VMEM((every, cols), bf16),
            pltpu.VMEM((every, cols), bf16),
            pltpu.VMEM((every, cols), f32),
            pltpu.VMEM((n_ctx - 1, rows, cols), bf16),
            pltpu.VMEM((n_ctx - 1, rows, cols), bf16),
            pltpu.VMEM((rows + 16, cols), f32),
            dma((9,)),
            dma((n_ctx - 1,)),
            dma((n_ctx - 1,)),
            dma((n_ctx - 1,)),
            dma((n_ctx - 1,)),
            dma((n_ctx - 1,)),
            dma((n_ctx - 1,)),
            dma((6,)),
            dma((6,)),
            dma((6,)),
            dma((6,)),
            dma((2,)),
            dma((n_ctx,)),
            dma((n_ctx,)),
            dma((n_ctx - 1,)),
            dma((n_ctx - 1,)),
        ],
        compiler_params=pltpu.CompilerParams(
            collective_id=0, has_side_effects=True, vmem_limit_bytes=60 * 1024 * 1024
        ),
    )(
        block_mask[0],
        tokens.reshape(rows, width),
        norm_gain[None],
        conv_weight,
        w_query,
        w_key,
        w_value,
        w_up,
        w_out,
        w_down,
    )
    return out.reshape(frames_here, dancers_here, cols)


def solution(mesh):
    def body(tokens, norm_gain, block_mask, w_query, *rest):
        n_ctx = mesh.shape["ctx"]
        pairs = all(mesh.shape[axis] == 2 for axis in ("groups", "tm", "tp"))
        split = w_query.shape[1] % (128 * n_ctx) == 0 and tokens.shape[1] * (KERNEL // 2) <= 8
        if pairs and split and n_ctx > 2:
            return in_one_kernel(n_ctx, tokens, norm_gain, block_mask, w_query, *rest)
        return on_device(tokens, norm_gain, block_mask, w_query, *rest)

    placed = (
        P(("groups", "tm"), "ctx", None),
        P(),
        P(("groups", "tm"), "ctx", None),
        P("tm", "tp"),
        P("tm", "tp"),
        P("tm", "tp"),
        P("tp", "tm"),
        P("tm", "tp"),
        P("tp", "tm"),
        P(None, "tp"),
    )
    return jax.shard_map(
        body,
        mesh=mesh,
        in_specs=placed,
        out_specs=P(("groups", "tm"), "ctx", "tp"),
        check_vma=False,
    )
```

```python
import functools

import jax
import jax.numpy as jnp
from jax import lax
from jax.experimental import pallas as pl
from jax.experimental.pallas import tpu as pltpu
from jax.sharding import PartitionSpec as P

HEAD_DIM = 64
KERNEL = 5


def from_behind(value, axis, steps):
    count = lax.axis_size(axis)
    first, last = (max(0, -steps), min(count, count - steps))
    return lax.ppermute(value, axis, [(source, source + steps) for source in range(first, last)])


def rms_norm(tokens, norm_gain):
    values = tokens.astype(jnp.float32)
    square = jnp.mean(values * values, axis=-1, keepdims=True)
    return (values * lax.rsqrt(square + 1e-05) * norm_gain).astype(jnp.bfloat16)


def on_device(
    tokens, norm_gain, block_mask, w_query, w_key, w_value, w_out, w_up, w_down, conv_weight
):
    frames_here, dancers_here, width = tokens.shape
    rows_here = frames_here * dancers_here
    normed_grid = rms_norm(tokens, norm_gain)
    normed = normed_grid.reshape(rows_here, width)
    pieces = (
        lax.all_gather(w_query, "tm", axis=0, tiled=True),
        lax.all_gather(w_key, "tm", axis=0, tiled=True),
        lax.all_gather(w_value, "tm", axis=0, tiled=True),
        lax.all_gather(w_up, "tm", axis=0, tiled=True),
    )
    query_sum, key_sum, value_sum, hidden = tuple(
        (jnp.dot(normed, piece_one, preferred_element_type=jnp.float32) for piece_one in pieces)
    )
    local_heads = query_sum.shape[1] // HEAD_DIM
    queries = query_sum.astype(jnp.bfloat16).reshape(rows_here, local_heads, HEAD_DIM)
    key_grid = key_sum.astype(jnp.bfloat16).reshape(
        frames_here, dancers_here, local_heads * HEAD_DIM
    )
    value_grid = value_sum.astype(jnp.bfloat16).reshape(
        frames_here, dancers_here, local_heads * HEAD_DIM
    )
    mask_row = block_mask[0, 0].astype(jnp.float32)
    cycle_blocks = mask_row.shape[0]
    key_piece = lax.all_gather(key_grid, "ctx", axis=1, tiled=True)
    value_piece = lax.all_gather(value_grid, "ctx", axis=1, tiled=True)
    count = key_piece.shape[1]
    block_ids = jnp.arange(count) // dancers_here
    picker = (block_ids[:, None] == jnp.arange(cycle_blocks)[None, :]).astype(jnp.float32)
    allowed_dancers = jnp.dot(picker, mask_row)
    peak_old = jnp.full((local_heads, rows_here), -1e30, jnp.float32)
    key_rows = key_piece.reshape(frames_here * count, local_heads, HEAD_DIM)
    value_rows = value_piece.reshape(frames_here * count, local_heads, HEAD_DIM)
    allowed = jnp.tile(allowed_dancers, frames_here)
    scores = (
        jnp.einsum("qhd,khd->hqk", queries, key_rows, preferred_element_type=jnp.float32) * 0.125
    )
    scores = jnp.where(allowed[None, None, :] > 0, scores, -1e30)
    peak_new = jnp.maximum(peak_old, jnp.max(scores, axis=-1))
    expo = jnp.exp(scores - peak_new[:, :, None]) * allowed[None, None, :]
    total_new = jnp.sum(expo, axis=-1)
    probs = expo.astype(jnp.bfloat16)
    mixed_new = jnp.einsum("hqk,khd->hqd", probs, value_rows, preferred_element_type=jnp.float32)
    attended = (
        (mixed_new / total_new[:, :, None])
        .transpose(1, 0, 2)
        .reshape(rows_here, local_heads * HEAD_DIM)
        .astype(jnp.bfloat16)
    )
    activated = jax.nn.gelu(hidden, approximate=True).astype(jnp.bfloat16)
    out_full, down_full = (
        lax.all_gather(w_out, "tm", axis=1, tiled=True),
        lax.all_gather(w_down, "tm", axis=1, tiled=True),
    )
    branches = jnp.dot(attended, out_full, preferred_element_type=jnp.float32)
    branches = branches + jnp.dot(activated, down_full, preferred_element_type=jnp.float32)
    mine = lax.psum_scatter(
        branches.astype(jnp.bfloat16), "tp", scatter_dimension=1, tiled=True
    ).astype(jnp.float32)
    features_here = mine.shape[1]
    first_feature = lax.axis_index("tp") * features_here
    normed_cols = lax.dynamic_slice_in_dim(normed_grid, first_feature, features_here, 2)
    padded = jnp.pad(normed_cols.astype(jnp.float32), ((4, 4), (0, 0), (0, 0)))
    extended = jnp.zeros((frames_here + 4, dancers_here, features_here), jnp.float32)
    for offset in range(KERNEL):
        extended = extended + conv_weight[offset] * padded[offset : offset + frames_here + 4]
    convolved = extended[2 : frames_here + 2]
    from_before = from_behind(extended[frames_here + 2 :], "tm", 1)
    from_after = from_behind(extended[0:2], "tm", -1)
    convolved = convolved.at[0:2].add(from_before)
    convolved = convolved.at[frames_here - 2 :].add(from_after)
    token_cols = lax.dynamic_slice_in_dim(tokens, first_feature, features_here, 2).astype(
        jnp.float32
    )
    result = token_cols + mine.reshape(frames_here, dancers_here, features_here) + convolved
    return result.astype(jnp.bfloat16)


MESH = pl.DeviceIdType.MESH


def normalised(values, gain):
    values = values.astype(jnp.float32)
    square = jnp.mean(values * values, axis=-1, keepdims=True)
    return (values * lax.rsqrt(square + 1e-05) * gain).astype(jnp.bfloat16)


def layer_kernel(
    n_ctx,
    frame,
    mask_ref,
    tokens_hbm,
    gain_hbm,
    conv_hbm,
    wq_ref,
    wk_ref,
    wv_ref,
    wup_ref,
    wout_ref,
    wdown_ref,
    out_ref,
    gain_ref,
    conv_ref,
    tok_all,
    normed,
    halo,
    halo_normed,
    bias,
    w_in,
    w_back,
    qkv,
    feats,
    theirs,
    sibling,
    mine,
    summed,
    arrived,
    extended,
    local_sem,
    tok_send,
    tok_recv,
    fwd_send,
    fwd_recv,
    bias_send,
    bias_recv,
    x_send,
    x_recv,
    y_send,
    y_recv,
    halo_sem,
    sib_send,
    sib_recv,
    red_send,
    red_recv,
):
    g = lax.axis_index("groups")
    c = lax.axis_index("ctx")
    i = lax.axis_index("tm")
    j = lax.axis_index("tp")
    rows, width = tokens_hbm.shape
    half_rows = rows // 2
    depth = wq_ref.shape[0]
    part = depth // 2
    hw = wq_ref.shape[1] // n_ctx
    fw = wup_ref.shape[1] // n_ctx
    cols = out_ref.shape[1]
    heads = hw // HEAD_DIM
    to_x = {"tm": 1 - i}
    to_y = {"groups": 1 - g}
    to_tp = {"tp": 1 - j}

    def ahead(step):
        return lax.rem(c + step, n_ctx)

    def behind(step):
        return lax.rem(c + n_ctx - step, n_ctx)

    pieces = []
    for block in range(n_ctx):
        term = (mask_ref[0, block].astype(jnp.float32) - 1.0) * 1e30
        pieces.append(jnp.full((8, rows), term, jnp.float32))
    bias[c] = jnp.concatenate(pieces, axis=1)

    barrier = pltpu.get_barrier_semaphore()
    for peer in (to_x, to_y, to_tp):
        pl.semaphore_signal(barrier, inc=1, device_id=peer, device_id_type=MESH)
    for step in range(1, n_ctx):
        pl.semaphore_signal(
            barrier, inc=1, device_id={"ctx": ahead(step)}, device_id_type=MESH
        )

    def rows_at(start, size):
        return pl.ds(pl.multiple_of(start, 16), size)

    def cols_at(start, size):
        return pl.ds(pl.multiple_of(start, 128), size)

    def slices(first, count, owner):
        out = []
        for index, ref in enumerate((wq_ref, wk_ref, wv_ref)):
            out.append(
                (
                    ref.at[rows_at(first * depth // 2, count * part), cols_at(c * hw, hw)],
                    w_in.at[
                        rows_at(owner * depth + first * part, count * part),
                        index * hw : (index + 1) * hw,
                    ],
                )
            )
        out.append(
            (
                wup_ref.at[rows_at(first * part, count * part), cols_at(c * fw, fw)],
                w_in.at[
                    rows_at(owner * depth + first * part, count * part),
                    3 * hw : 3 * hw + fw,
                ],
            )
        )
        out.append(
            (
                wout_ref.at[rows_at(c * hw + first * (hw // 2), count * (hw // 2)), :],
                w_back.at[
                    rows_at(first * (hw // 2), count * (hw // 2)),
                    cols_at(owner * cols, cols),
                ],
            )
        )
        out.append(
            (
                wdown_ref.at[rows_at(c * fw + first * (fw // 2), count * (fw // 2)), :],
                w_back.at[
                    rows_at(hw + first * (fw // 2), count * (fw // 2)),
                    cols_at(owner * cols, cols),
                ],
            )
        )
        return out

    local = [
        pltpu.make_async_copy(source, target, local_sem.at[index])
        for index, (source, target) in enumerate(slices(0, 2, i))
    ]
    local.append(
        pltpu.make_async_copy(
            tokens_hbm, tok_all.at[rows_at(c * rows, rows)], local_sem.at[6]
        )
    )
    local.append(pltpu.make_async_copy(gain_hbm, gain_ref, local_sem.at[7]))
    local.append(pltpu.make_async_copy(conv_hbm, conv_ref, local_sem.at[8]))
    for copy in local:
        copy.start()
    pl.semaphore_wait(barrier, n_ctx + 2)

    def remote(source, target, send, recv, peer):
        return pltpu.make_async_remote_copy(
            src_ref=source,
            dst_ref=target,
            send_sem=send,
            recv_sem=recv,
            device_id=peer,
            device_id_type=MESH,
        )

    x_out = [
        remote(source, target, x_send.at[index], x_recv.at[index], to_x)
        for index, (source, target) in enumerate(slices(g, 1, i))
    ]
    x_in = [
        remote(source, target, x_send.at[index], x_recv.at[index], to_x)
        for index, (source, target) in enumerate(slices(g, 1, 1 - i))
    ]
    halo_copy = remote(
        tokens_hbm.at[rows_at((1 - i) * (rows - 16), 16)],
        halo,
        halo_sem.at[0],
        halo_sem.at[1],
        to_x,
    )

    def token_half(block, half):
        return tok_all.at[rows_at(block * rows + half * half_rows, half_rows)]

    tok_out, tok_in, fwd_out, fwd_in, bias_out, bias_in = [], [], [], [], [], []
    for step in range(1, n_ctx):
        peer = {"ctx": ahead(step)}
        at = step - 1
        own_half = tokens_hbm.at[rows_at(j * half_rows, half_rows)]
        tok_out.append(
            remote(own_half, token_half(c, j), tok_send.at[at], tok_recv.at[at], peer)
        )
        source = behind(step)
        tok_in.append(
            remote(own_half, token_half(source, j), tok_send.at[at], tok_recv.at[at], peer)
        )
        fwd_out.append(
            remote(
                token_half(source, j), token_half(source, j), fwd_send.at[at], fwd_recv.at[at], to_tp
            )
        )
        fwd_in.append(
            remote(
                token_half(source, 1 - j),
                token_half(source, 1 - j),
                fwd_send.at[at],
                fwd_recv.at[at],
                to_tp,
            )
        )
        bias_out.append(remote(bias.at[c], bias.at[c], bias_send.at[at], bias_recv.at[at], peer))
        bias_in.append(
            remote(bias.at[source], bias.at[source], bias_send.at[at], bias_recv.at[at], peer)
        )

    def y_copies(half):
        return [
            remote(target, target, y_send.at[index], y_recv.at[index], to_y)
            for index, (_, target) in enumerate(slices(half, 1, 1 - i))
        ]

    y_out, y_in = y_copies(g), y_copies(1 - g)

    steps = [2, 1] + list(range(3, n_ctx))
    for step in steps:
        tok_out[step - 1].start()
    for copy in x_out[:4]:
        copy.start()
    halo_copy.start()
    for copy in x_out[4:]:
        copy.start()
    for copy in bias_out:
        copy.start()

    local[7].wait()
    gain = gain_ref[...]

    def norm_block(block):
        at = rows_at(block * rows, rows)
        normed[at, :] = normalised(tok_all[at, :], gain)

    local[6].wait()
    norm_block(c)

    def pass_on(index):
        x_in[index].wait_recv()
        y_out[index].start()

    def share(step):
        tok_in[step - 1].wait_recv()
        fwd_out[step - 1].start()

    def settle(step):
        fwd_in[step - 1].wait_recv()
        norm_block(behind(step))

    def project(block):
        at = rows_at(block * rows, rows)
        qkv[at, :] = jnp.dot(
            normed[at, :], w_in[:, 0 : 3 * hw], preferred_element_type=jnp.float32
        ).astype(jnp.bfloat16)

    def feed(block):
        at = rows_at(block * rows, rows)
        hidden = jnp.dot(
            normed[at, :], w_in[:, 3 * hw : 3 * hw + fw], preferred_element_type=jnp.float32
        )
        feats[at, hw : hw + fw] = jax.nn.gelu(hidden, approximate=True).astype(jnp.bfloat16)

    def attend(block):
        at = rows_at(block * rows, rows)
        outs = []
        for head in range(heads):
            low = head * HEAD_DIM
            query = qkv[at, low : low + HEAD_DIM]
            key = qkv[:, hw + low : hw + low + HEAD_DIM]
            value = qkv[:, 2 * hw + low : 2 * hw + low + HEAD_DIM]
            scores = lax.dot_general(
                query, key, (((1,), (1,)), ((), ())), preferred_element_type=jnp.float32
            )
            scores = scores * 0.125 + bias[block][0:1, :]
            peak = jnp.max(scores, axis=-1, keepdims=True)
            expo = jnp.exp(scores - peak)
            total = jnp.sum(expo, axis=-1, keepdims=True)
            mixed = jnp.dot(
                expo.astype(jnp.bfloat16), value, preferred_element_type=jnp.float32
            )
            outs.append(mixed / total)
        feats[at, 0:hw] = jnp.concatenate(outs, axis=1).astype(jnp.bfloat16)

    pass_on(0)
    pass_on(1)
    pass_on(2)
    share(steps[0])
    pass_on(3)
    share(steps[1])
    settle(steps[0])
    for copy in local[:4]:
        copy.wait()
    for copy in y_in[:3]:
        copy.wait_recv()
    project(c)
    pass_on(4)
    project(behind(steps[0]))
    settle(steps[1])
    project(behind(steps[1]))
    y_in[3].wait_recv()
    feed(c)
    pass_on(5)
    for step in steps[2:]:
        share(step)
    feed(behind(steps[0]))
    feed(behind(steps[1]))
    for step in steps[2:]:
        settle(step)
        project(behind(step))
        feed(behind(step))
    for copy in bias_in:
        copy.wait_recv()
    for copy in local[4:6]:
        copy.wait()

    order = steps + [0]
    sib, red = [], []
    for index, step in enumerate(order):
        at = rows_at(ahead(step) * rows, rows)
        sib.append(
            remote(theirs.at[at], sibling.at[at], sib_send.at[index], sib_recv.at[index], to_tp)
        )
        if step > 0:
            red.append(
                remote(
                    summed.at[step - 1],
                    arrived.at[step - 1],
                    red_send.at[step - 1],
                    red_recv.at[step - 1],
                    {"ctx": ahead(step)},
                )
            )

    def product(index, half):
        at = rows_at(ahead(order[index]) * rows, rows)
        return jnp.dot(
            feats[at, :], w_back[:, cols_at(half * cols, cols)], preferred_element_type=jnp.float32
        )

    def give(index, half):
        at = rows_at(ahead(order[index]) * rows, rows)
        theirs[at, :] = product(index, half).astype(jnp.bfloat16)
        sib[index].start()

    def keep(index, half):
        at = rows_at(ahead(order[index]) * rows, rows)
        mine[at, :] = product(index, half)

    def reduce(index):
        step = order[index]
        at = rows_at(ahead(step) * rows, rows)
        sib[index].wait_recv()
        summed[step - 1] = (mine[at, :] + sibling[at, :].astype(jnp.float32)).astype(jnp.bfloat16)
        red[index].start()

    for index, step in enumerate(order):
        attend(ahead(step))

        @pl.when(j != i)
        def _(index=index):
            give(index, i)

        @pl.when(j == i)
        def _(index=index):
            keep(index, i)
            if index > 0:
                reduce(index - 1)

    y_in[4].wait_recv()
    y_in[5].wait_recv()
    for index in range(n_ctx):

        @pl.when(j == i)
        def _(index=index):
            give(index, 1 - i)

        @pl.when(j != i)
        def _(index=index):
            keep(index, 1 - i)
            if index > 0:
                reduce(index - 1)

    local[8].wait()
    halo_copy.wait_recv()
    halo_normed[...] = normalised(halo[...], gain)
    edge = halo_normed[:, cols_at(j * cols, cols)].astype(jnp.float32)
    own = rows_at(c * rows, rows)
    my_cols = cols_at(j * cols, cols)
    reach = KERNEL // 2
    before = jnp.where(i == 1, edge[8:16], 0.0)
    after = jnp.where(i == 0, edge[0:8], 0.0)
    extended[0:8, :] = before
    extended[8 : 8 + rows, :] = normed[own, my_cols].astype(jnp.float32)
    extended[8 + rows : 16 + rows, :] = after
    base = tok_all[own, my_cols].astype(jnp.float32)
    for tap in range(KERNEL):
        shift = 8 + (tap - reach) * frame
        base = base + conv_ref[tap : tap + 1, :] * extended[shift : shift + rows, :]
    sib[n_ctx - 1].wait_recv()
    base = base + mine[own, :] + sibling[own, :].astype(jnp.float32)
    for copy in red:
        copy.wait_recv()
    for step in range(n_ctx - 1):
        base = base + arrived[step].astype(jnp.float32)
    out_ref[...] = base.astype(out_ref.dtype)

    for copy in tok_out + x_out + [halo_copy] + bias_out + fwd_out + y_out + sib + red:
        copy.wait_send()


def in_one_kernel(
    n_ctx, tokens, norm_gain, block_mask, w_query, w_key, w_value, w_out, w_up, w_down, conv_weight
):
    frames_here, dancers_here, width = tokens.shape
    rows = frames_here * dancers_here
    cols = w_out.shape[1]
    hw = w_query.shape[1] // n_ctx
    fw = w_up.shape[1] // n_ctx
    depth = w_query.shape[0]
    every = n_ctx * rows
    bf16, f32 = jnp.bfloat16, jnp.float32
    vmem = pl.BlockSpec(memory_space=pltpu.VMEM)
    hbm = pl.BlockSpec(memory_space=pl.ANY)
    dma = pltpu.SemaphoreType.DMA
    out = pl.pallas_call(
        functools.partial(layer_kernel, n_ctx, dancers_here),
        out_shape=jax.ShapeDtypeStruct((rows, cols), bf16),
        in_specs=[pl.BlockSpec(memory_space=pltpu.SMEM)] + [hbm] * 9,
        out_specs=vmem,
        scratch_shapes=[
            pltpu.VMEM((1, width), f32),
            pltpu.VMEM(conv_weight.shape, f32),
            pltpu.VMEM((every, width), bf16),
            pltpu.VMEM((every, width), bf16),
            pltpu.VMEM((16, width), bf16),
            pltpu.VMEM((16, width), bf16),
            pltpu.VMEM((n_ctx, 8, every), f32),
            pltpu.VMEM((2 * depth, 3 * hw + fw), bf16),
            pltpu.VMEM((hw + fw, 2 * cols), bf16),
            pltpu.VMEM((every, 3 * hw), bf16),
            pltpu.VMEM((every, hw + fw), bf16),
            pltpu.VMEM((every, cols), bf16),
            pltpu.VMEM((every, cols), bf16),
            pltpu.VMEM((every, cols), f32),
            pltpu.VMEM((n_ctx - 1, rows, cols), bf16),
            pltpu.VMEM((n_ctx - 1, rows, cols), bf16),
            pltpu.VMEM((rows + 16, cols), f32),
            dma((9,)),
            dma((n_ctx - 1,)),
            dma((n_ctx - 1,)),
            dma((n_ctx - 1,)),
            dma((n_ctx - 1,)),
            dma((n_ctx - 1,)),
            dma((n_ctx - 1,)),
            dma((6,)),
            dma((6,)),
            dma((6,)),
            dma((6,)),
            dma((2,)),
            dma((n_ctx,)),
            dma((n_ctx,)),
            dma((n_ctx - 1,)),
            dma((n_ctx - 1,)),
        ],
        compiler_params=pltpu.CompilerParams(
            collective_id=0, has_side_effects=True, vmem_limit_bytes=60 * 1024 * 1024
        ),
    )(
        block_mask[0],
        tokens.reshape(rows, width),
        norm_gain[None],
        conv_weight,
        w_query,
        w_key,
        w_value,
        w_up,
        w_out,
        w_down,
    )
    return out.reshape(frames_here, dancers_here, cols)


def solution(mesh):
    def body(tokens, norm_gain, block_mask, w_query, *rest):
        n_ctx = mesh.shape["ctx"]
        pairs = all(mesh.shape[axis] == 2 for axis in ("groups", "tm", "tp"))
        split = w_query.shape[1] % (128 * n_ctx) == 0 and tokens.shape[1] * (KERNEL // 2) <= 8
        if pairs and split and n_ctx > 2:
            return in_one_kernel(n_ctx, tokens, norm_gain, block_mask, w_query, *rest)
        return on_device(tokens, norm_gain, block_mask, w_query, *rest)

    placed = (
        P(("groups", "tm"), "ctx", None),
        P(),
        P(("groups", "tm"), "ctx", None),
        P("tm", "tp"),
        P("tm", "tp"),
        P("tm", "tp"),
        P("tp", "tm"),
        P("tm", "tp"),
        P("tp", "tm"),
        P(None, "tp"),
    )
    return jax.shard_map(
        body,
        mesh=mesh,
        in_specs=placed,
        out_specs=P(("groups", "tm"), "ctx", "tp"),
        check_vma=False,
    )
```

```python
import functools

import jax
import jax.numpy as jnp
from jax import lax
from jax.experimental import pallas as pl
from jax.experimental.pallas import tpu as pltpu
from jax.sharding import PartitionSpec as P

HEAD_DIM = 64
KERNEL = 5


def from_behind(value, axis, steps):
    count = lax.axis_size(axis)
    first, last = (max(0, -steps), min(count, count - steps))
    return lax.ppermute(value, axis, [(source, source + steps) for source in range(first, last)])


def rms_norm(tokens, norm_gain):
    values = tokens.astype(jnp.float32)
    square = jnp.mean(values * values, axis=-1, keepdims=True)
    return (values * lax.rsqrt(square + 1e-05) * norm_gain).astype(jnp.bfloat16)


def on_device(
    tokens, norm_gain, block_mask, w_query, w_key, w_value, w_out, w_up, w_down, conv_weight
):
    frames_here, dancers_here, width = tokens.shape
    rows_here = frames_here * dancers_here
    normed_grid = rms_norm(tokens, norm_gain)
    normed = normed_grid.reshape(rows_here, width)
    pieces = (
        lax.all_gather(w_query, "tm", axis=0, tiled=True),
        lax.all_gather(w_key, "tm", axis=0, tiled=True),
        lax.all_gather(w_value, "tm", axis=0, tiled=True),
        lax.all_gather(w_up, "tm", axis=0, tiled=True),
    )
    query_sum, key_sum, value_sum, hidden = tuple(
        (jnp.dot(normed, piece_one, preferred_element_type=jnp.float32) for piece_one in pieces)
    )
    local_heads = query_sum.shape[1] // HEAD_DIM
    queries = query_sum.astype(jnp.bfloat16).reshape(rows_here, local_heads, HEAD_DIM)
    key_grid = key_sum.astype(jnp.bfloat16).reshape(
        frames_here, dancers_here, local_heads * HEAD_DIM
    )
    value_grid = value_sum.astype(jnp.bfloat16).reshape(
        frames_here, dancers_here, local_heads * HEAD_DIM
    )
    mask_row = block_mask[0, 0].astype(jnp.float32)
    cycle_blocks = mask_row.shape[0]
    key_piece = lax.all_gather(key_grid, "ctx", axis=1, tiled=True)
    value_piece = lax.all_gather(value_grid, "ctx", axis=1, tiled=True)
    count = key_piece.shape[1]
    block_ids = jnp.arange(count) // dancers_here
    picker = (block_ids[:, None] == jnp.arange(cycle_blocks)[None, :]).astype(jnp.float32)
    allowed_dancers = jnp.dot(picker, mask_row)
    peak_old = jnp.full((local_heads, rows_here), -1e30, jnp.float32)
    key_rows = key_piece.reshape(frames_here * count, local_heads, HEAD_DIM)
    value_rows = value_piece.reshape(frames_here * count, local_heads, HEAD_DIM)
    allowed = jnp.tile(allowed_dancers, frames_here)
    scores = (
        jnp.einsum("qhd,khd->hqk", queries, key_rows, preferred_element_type=jnp.float32) * 0.125
    )
    scores = jnp.where(allowed[None, None, :] > 0, scores, -1e30)
    peak_new = jnp.maximum(peak_old, jnp.max(scores, axis=-1))
    expo = jnp.exp(scores - peak_new[:, :, None]) * allowed[None, None, :]
    total_new = jnp.sum(expo, axis=-1)
    probs = expo.astype(jnp.bfloat16)
    mixed_new = jnp.einsum("hqk,khd->hqd", probs, value_rows, preferred_element_type=jnp.float32)
    attended = (
        (mixed_new / total_new[:, :, None])
        .transpose(1, 0, 2)
        .reshape(rows_here, local_heads * HEAD_DIM)
        .astype(jnp.bfloat16)
    )
    activated = jax.nn.gelu(hidden, approximate=True).astype(jnp.bfloat16)
    out_full, down_full = (
        lax.all_gather(w_out, "tm", axis=1, tiled=True),
        lax.all_gather(w_down, "tm", axis=1, tiled=True),
    )
    branches = jnp.dot(attended, out_full, preferred_element_type=jnp.float32)
    branches = branches + jnp.dot(activated, down_full, preferred_element_type=jnp.float32)
    mine = lax.psum_scatter(
        branches.astype(jnp.bfloat16), "tp", scatter_dimension=1, tiled=True
    ).astype(jnp.float32)
    features_here = mine.shape[1]
    first_feature = lax.axis_index("tp") * features_here
    normed_cols = lax.dynamic_slice_in_dim(normed_grid, first_feature, features_here, 2)
    padded = jnp.pad(normed_cols.astype(jnp.float32), ((4, 4), (0, 0), (0, 0)))
    extended = jnp.zeros((frames_here + 4, dancers_here, features_here), jnp.float32)
    for offset in range(KERNEL):
        extended = extended + conv_weight[offset] * padded[offset : offset + frames_here + 4]
    convolved = extended[2 : frames_here + 2]
    from_before = from_behind(extended[frames_here + 2 :], "tm", 1)
    from_after = from_behind(extended[0:2], "tm", -1)
    convolved = convolved.at[0:2].add(from_before)
    convolved = convolved.at[frames_here - 2 :].add(from_after)
    token_cols = lax.dynamic_slice_in_dim(tokens, first_feature, features_here, 2).astype(
        jnp.float32
    )
    result = token_cols + mine.reshape(frames_here, dancers_here, features_here) + convolved
    return result.astype(jnp.bfloat16)


MESH = pl.DeviceIdType.MESH


def normalised(values, gain):
    values = values.astype(jnp.float32)
    square = jnp.mean(values * values, axis=-1, keepdims=True)
    return (values * lax.rsqrt(square + 1e-05) * gain).astype(jnp.bfloat16)


def layer_kernel(
    n_ctx,
    frame,
    mask_ref,
    tokens_hbm,
    gain_hbm,
    conv_hbm,
    wq_ref,
    wk_ref,
    wv_ref,
    wup_ref,
    wout_ref,
    wdown_ref,
    out_ref,
    gain_ref,
    conv_ref,
    tok_all,
    normed,
    halo,
    halo_normed,
    bias,
    w_in,
    w_back,
    qkv,
    feats,
    theirs,
    sibling,
    mine,
    summed,
    arrived,
    extended,
    local_sem,
    tok_send,
    tok_recv,
    fwd_send,
    fwd_recv,
    bias_send,
    bias_recv,
    x_send,
    x_recv,
    y_send,
    y_recv,
    halo_sem,
    sib_send,
    sib_recv,
    red_send,
    red_recv,
):
    g = lax.axis_index("groups")
    c = lax.axis_index("ctx")
    i = lax.axis_index("tm")
    j = lax.axis_index("tp")
    rows, width = tokens_hbm.shape
    half_rows = rows // 2
    depth = wq_ref.shape[0]
    part = depth // 2
    hw = wq_ref.shape[1] // n_ctx
    fw = wup_ref.shape[1] // n_ctx
    cols = out_ref.shape[1]
    heads = hw // HEAD_DIM
    to_x = {"tm": 1 - i}
    to_y = {"groups": 1 - g}
    to_tp = {"tp": 1 - j}

    def ahead(step):
        return lax.rem(c + step, n_ctx)

    def behind(step):
        return lax.rem(c + n_ctx - step, n_ctx)

    pieces = []
    for block in range(n_ctx):
        term = (mask_ref[0, block].astype(jnp.float32) - 1.0) * 1e30
        pieces.append(jnp.full((8, rows), term, jnp.float32))
    bias[c] = jnp.concatenate(pieces, axis=1)

    barrier = pltpu.get_barrier_semaphore()
    for peer in (to_x, to_y, to_tp):
        pl.semaphore_signal(barrier, inc=1, device_id=peer, device_id_type=MESH)
    for step in range(1, n_ctx):
        pl.semaphore_signal(
            barrier, inc=1, device_id={"ctx": ahead(step)}, device_id_type=MESH
        )

    def rows_at(start, size):
        return pl.ds(pl.multiple_of(start, 16), size)

    def cols_at(start, size):
        return pl.ds(pl.multiple_of(start, 128), size)

    def slices(first, count, owner):
        out = []
        for index, ref in enumerate((wq_ref, wk_ref, wv_ref)):
            out.append(
                (
                    ref.at[rows_at(first * depth // 2, count * part), cols_at(c * hw, hw)],
                    w_in.at[
                        rows_at(owner * depth + first * part, count * part),
                        index * hw : (index + 1) * hw,
                    ],
                )
            )
        out.append(
            (
                wup_ref.at[rows_at(first * part, count * part), cols_at(c * fw, fw)],
                w_in.at[
                    rows_at(owner * depth + first * part, count * part),
                    3 * hw : 3 * hw + fw,
                ],
            )
        )
        out.append(
            (
                wout_ref.at[rows_at(c * hw + first * (hw // 2), count * (hw // 2)), :],
                w_back.at[
                    rows_at(first * (hw // 2), count * (hw // 2)),
                    cols_at(owner * cols, cols),
                ],
            )
        )
        quarter = count * (fw // 2) // 2
        for piece in range(2):
            start = first * (fw // 2) + piece * quarter
            out.append(
                (
                    wdown_ref.at[rows_at(c * fw + start, quarter), :],
                    w_back.at[rows_at(hw + start, quarter), cols_at(owner * cols, cols)],
                )
            )
        return out

    local = [
        pltpu.make_async_copy(source, target, local_sem.at[index])
        for index, (source, target) in enumerate(slices(0, 2, i))
    ]
    local.append(
        pltpu.make_async_copy(
            tokens_hbm, tok_all.at[rows_at(c * rows, rows)], local_sem.at[7]
        )
    )
    local.append(pltpu.make_async_copy(gain_hbm, gain_ref, local_sem.at[8]))
    local.append(pltpu.make_async_copy(conv_hbm, conv_ref, local_sem.at[9]))
    for copy in local:
        copy.start()
    pl.semaphore_wait(barrier, n_ctx + 2)

    def remote(source, target, send, recv, peer):
        return pltpu.make_async_remote_copy(
            src_ref=source,
            dst_ref=target,
            send_sem=send,
            recv_sem=recv,
            device_id=peer,
            device_id_type=MESH,
        )

    x_out = [
        remote(source, target, x_send.at[index], x_recv.at[index], to_x)
        for index, (source, target) in enumerate(slices(g, 1, i))
    ]
    x_in = [
        remote(source, target, x_send.at[index], x_recv.at[index], to_x)
        for index, (source, target) in enumerate(slices(g, 1, 1 - i))
    ]
    halo_copy = remote(
        tokens_hbm.at[rows_at((1 - i) * (rows - 16), 16)],
        halo,
        halo_sem.at[0],
        halo_sem.at[1],
        to_x,
    )

    def token_half(block, half):
        return tok_all.at[rows_at(block * rows + half * half_rows, half_rows)]

    tok_out, tok_in, fwd_out, fwd_in, bias_out, bias_in = [], [], [], [], [], []
    for step in range(1, n_ctx):
        peer = {"ctx": ahead(step)}
        at = step - 1
        own_half = tokens_hbm.at[rows_at(j * half_rows, half_rows)]
        tok_out.append(
            remote(own_half, token_half(c, j), tok_send.at[at], tok_recv.at[at], peer)
        )
        source = behind(step)
        tok_in.append(
            remote(own_half, token_half(source, j), tok_send.at[at], tok_recv.at[at], peer)
        )
        fwd_out.append(
            remote(
                token_half(source, j), token_half(source, j), fwd_send.at[at], fwd_recv.at[at], to_tp
            )
        )
        fwd_in.append(
            remote(
                token_half(source, 1 - j),
                token_half(source, 1 - j),
                fwd_send.at[at],
                fwd_recv.at[at],
                to_tp,
            )
        )
        bias_out.append(remote(bias.at[c], bias.at[c], bias_send.at[at], bias_recv.at[at], peer))
        bias_in.append(
            remote(bias.at[source], bias.at[source], bias_send.at[at], bias_recv.at[at], peer)
        )

    def y_copies(half):
        return [
            remote(target, target, y_send.at[index], y_recv.at[index], to_y)
            for index, (_, target) in enumerate(slices(half, 1, 1 - i))
        ]

    y_out, y_in = y_copies(g), y_copies(1 - g)

    steps = [2, 1] + list(range(3, n_ctx))
    for step in steps:
        tok_out[step - 1].start()
    for copy in x_out[:4]:
        copy.start()
    halo_copy.start()
    for copy in x_out[4:]:
        copy.start()
    for copy in bias_out:
        copy.start()

    local[8].wait()
    gain = gain_ref[...]

    def norm_block(block):
        at = rows_at(block * rows, rows)
        normed[at, :] = normalised(tok_all[at, :], gain)

    local[7].wait()
    norm_block(c)

    def pass_on(index):
        x_in[index].wait_recv()
        y_out[index].start()

    def share(step):
        tok_in[step - 1].wait_recv()
        fwd_out[step - 1].start()

    def settle(step):
        fwd_in[step - 1].wait_recv()
        norm_block(behind(step))

    def project(block):
        at = rows_at(block * rows, rows)
        qkv[at, :] = jnp.dot(
            normed[at, :], w_in[:, 0 : 3 * hw], preferred_element_type=jnp.float32
        ).astype(jnp.bfloat16)

    def feed(block):
        at = rows_at(block * rows, rows)
        hidden = jnp.dot(
            normed[at, :], w_in[:, 3 * hw : 3 * hw + fw], preferred_element_type=jnp.float32
        )
        feats[at, hw : hw + fw] = jax.nn.gelu(hidden, approximate=True).astype(jnp.bfloat16)

    def attend(block):
        at = rows_at(block * rows, rows)
        outs = []
        for head in range(heads):
            low = head * HEAD_DIM
            query = qkv[at, low : low + HEAD_DIM]
            key = qkv[:, hw + low : hw + low + HEAD_DIM]
            value = qkv[:, 2 * hw + low : 2 * hw + low + HEAD_DIM]
            scores = lax.dot_general(
                query, key, (((1,), (1,)), ((), ())), preferred_element_type=jnp.float32
            )
            scores = scores * 0.125 + bias[block][0:1, :]
            peak = jnp.max(scores, axis=-1, keepdims=True)
            expo = jnp.exp(scores - peak)
            total = jnp.sum(expo, axis=-1, keepdims=True)
            mixed = jnp.dot(
                expo.astype(jnp.bfloat16), value, preferred_element_type=jnp.float32
            )
            outs.append(mixed / total)
        feats[at, 0:hw] = jnp.concatenate(outs, axis=1).astype(jnp.bfloat16)

    pass_on(0)
    pass_on(1)
    pass_on(2)
    share(steps[0])
    pass_on(3)
    share(steps[1])
    settle(steps[0])
    for copy in local[:4]:
        copy.wait()
    for copy in y_in[:3]:
        copy.wait_recv()
    project(c)
    pass_on(4)
    project(behind(steps[0]))
    settle(steps[1])
    project(behind(steps[1]))
    y_in[3].wait_recv()
    feed(c)
    for step in steps[2:]:
        share(step)
    pass_on(5)
    feed(behind(steps[0]))
    feed(behind(steps[1]))
    for step in steps[2:]:
        settle(step)
        project(behind(step))
        feed(behind(step))
    pass_on(6)
    for copy in bias_in:
        copy.wait_recv()
    for copy in local[4:7]:
        copy.wait()

    order = steps + [0]
    sib, red = [], []
    for index, step in enumerate(order):
        at = rows_at(ahead(step) * rows, rows)
        sib.append(
            remote(theirs.at[at], sibling.at[at], sib_send.at[index], sib_recv.at[index], to_tp)
        )
        if step > 0:
            red.append(
                remote(
                    summed.at[step - 1],
                    arrived.at[step - 1],
                    red_send.at[step - 1],
                    red_recv.at[step - 1],
                    {"ctx": ahead(step)},
                )
            )

    def product(index, half):
        at = rows_at(ahead(order[index]) * rows, rows)
        return jnp.dot(
            feats[at, :], w_back[:, cols_at(half * cols, cols)], preferred_element_type=jnp.float32
        )

    def give(index, half):
        at = rows_at(ahead(order[index]) * rows, rows)
        theirs[at, :] = product(index, half).astype(jnp.bfloat16)
        sib[index].start()

    def keep(index, half):
        at = rows_at(ahead(order[index]) * rows, rows)
        mine[at, :] = product(index, half)

    def reduce(index):
        step = order[index]
        at = rows_at(ahead(step) * rows, rows)
        sib[index].wait_recv()
        summed[step - 1] = (mine[at, :] + sibling[at, :].astype(jnp.float32)).astype(jnp.bfloat16)
        red[index].start()

    for index, step in enumerate(order):
        attend(ahead(step))

        @pl.when(j != i)
        def _(index=index):
            give(index, i)

        @pl.when(j == i)
        def _(index=index):
            keep(index, i)
            if index > 0:
                reduce(index - 1)

    y_in[4].wait_recv()
    y_in[5].wait_recv()
    y_in[6].wait_recv()
    for index in range(n_ctx):

        @pl.when(j == i)
        def _(index=index):
            give(index, 1 - i)

        @pl.when(j != i)
        def _(index=index):
            keep(index, 1 - i)
            if index > 0:
                reduce(index - 1)

    local[9].wait()
    halo_copy.wait_recv()
    halo_normed[...] = normalised(halo[...], gain)
    edge = halo_normed[:, cols_at(j * cols, cols)].astype(jnp.float32)
    own = rows_at(c * rows, rows)
    my_cols = cols_at(j * cols, cols)
    reach = KERNEL // 2
    before = jnp.where(i == 1, edge[8:16], 0.0)
    after = jnp.where(i == 0, edge[0:8], 0.0)
    extended[0:8, :] = before
    extended[8 : 8 + rows, :] = normed[own, my_cols].astype(jnp.float32)
    extended[8 + rows : 16 + rows, :] = after
    base = tok_all[own, my_cols].astype(jnp.float32)
    for tap in range(KERNEL):
        shift = 8 + (tap - reach) * frame
        base = base + conv_ref[tap : tap + 1, :] * extended[shift : shift + rows, :]
    sib[n_ctx - 1].wait_recv()
    base = base + mine[own, :] + sibling[own, :].astype(jnp.float32)
    for copy in red:
        copy.wait_recv()
    for step in range(n_ctx - 1):
        base = base + arrived[step].astype(jnp.float32)
    out_ref[...] = base.astype(out_ref.dtype)

    for copy in tok_out + x_out + [halo_copy] + bias_out + fwd_out + y_out + sib + red:
        copy.wait_send()


def in_one_kernel(
    n_ctx, tokens, norm_gain, block_mask, w_query, w_key, w_value, w_out, w_up, w_down, conv_weight
):
    frames_here, dancers_here, width = tokens.shape
    rows = frames_here * dancers_here
    cols = w_out.shape[1]
    hw = w_query.shape[1] // n_ctx
    fw = w_up.shape[1] // n_ctx
    depth = w_query.shape[0]
    every = n_ctx * rows
    bf16, f32 = jnp.bfloat16, jnp.float32
    vmem = pl.BlockSpec(memory_space=pltpu.VMEM)
    hbm = pl.BlockSpec(memory_space=pl.ANY)
    dma = pltpu.SemaphoreType.DMA
    out = pl.pallas_call(
        functools.partial(layer_kernel, n_ctx, dancers_here),
        out_shape=jax.ShapeDtypeStruct((rows, cols), bf16),
        in_specs=[pl.BlockSpec(memory_space=pltpu.SMEM)] + [hbm] * 9,
        out_specs=vmem,
        scratch_shapes=[
            pltpu.VMEM((1, width), f32),
            pltpu.VMEM(conv_weight.shape, f32),
            pltpu.VMEM((every, width), bf16),
            pltpu.VMEM((every, width), bf16),
            pltpu.VMEM((16, width), bf16),
            pltpu.VMEM((16, width), bf16),
            pltpu.VMEM((n_ctx, 8, every), f32),
            pltpu.VMEM((2 * depth, 3 * hw + fw), bf16),
            pltpu.VMEM((hw + fw, 2 * cols), bf16),
            pltpu.VMEM((every, 3 * hw), bf16),
            pltpu.VMEM((every, hw + fw), bf16),
            pltpu.VMEM((every, cols), bf16),
            pltpu.VMEM((every, cols), bf16),
            pltpu.VMEM((every, cols), f32),
            pltpu.VMEM((n_ctx - 1, rows, cols), bf16),
            pltpu.VMEM((n_ctx - 1, rows, cols), bf16),
            pltpu.VMEM((rows + 16, cols), f32),
            dma((10,)),
            dma((n_ctx - 1,)),
            dma((n_ctx - 1,)),
            dma((n_ctx - 1,)),
            dma((n_ctx - 1,)),
            dma((n_ctx - 1,)),
            dma((n_ctx - 1,)),
            dma((7,)),
            dma((7,)),
            dma((7,)),
            dma((7,)),
            dma((2,)),
            dma((n_ctx,)),
            dma((n_ctx,)),
            dma((n_ctx - 1,)),
            dma((n_ctx - 1,)),
        ],
        compiler_params=pltpu.CompilerParams(
            collective_id=0, has_side_effects=True, vmem_limit_bytes=60 * 1024 * 1024
        ),
    )(
        block_mask[0],
        tokens.reshape(rows, width),
        norm_gain[None],
        conv_weight,
        w_query,
        w_key,
        w_value,
        w_up,
        w_out,
        w_down,
    )
    return out.reshape(frames_here, dancers_here, cols)


def solution(mesh):
    def body(tokens, norm_gain, block_mask, w_query, *rest):
        n_ctx = mesh.shape["ctx"]
        pairs = all(mesh.shape[axis] == 2 for axis in ("groups", "tm", "tp"))
        split = w_query.shape[1] % (128 * n_ctx) == 0 and tokens.shape[1] * (KERNEL // 2) <= 8
        if pairs and split and n_ctx > 2:
            return in_one_kernel(n_ctx, tokens, norm_gain, block_mask, w_query, *rest)
        return on_device(tokens, norm_gain, block_mask, w_query, *rest)

    placed = (
        P(("groups", "tm"), "ctx", None),
        P(),
        P(("groups", "tm"), "ctx", None),
        P("tm", "tp"),
        P("tm", "tp"),
        P("tm", "tp"),
        P("tp", "tm"),
        P("tm", "tp"),
        P("tp", "tm"),
        P(None, "tp"),
    )
    return jax.shard_map(
        body,
        mesh=mesh,
        in_specs=placed,
        out_specs=P(("groups", "tm"), "ctx", "tp"),
        check_vma=False,
    )
```
